512 devices in a mesh: tensor: 8 (over y, core), adapter: 16 (over z), dp: 4 (over x).
Axes of the slice: x: 4, y: 4, z: 16, core: 2. Of those that a mesh axis runs over, the one named last changes fastest.
Arguments:
- tokens: bfloat16 [16384, 8192], P(('adapter', 'dp'), 'tensor'), may hold values from -6 to 6
- base_projection_weight: bfloat16 [8192, 4096], P('tensor', 'dp'), may hold values from -0.0625 to 0.0625
- adapter_down_weight: bfloat16 [32, 8192, 64], P('adapter', 'tensor'), may hold values from -0.0625 to 0.0625
- adapter_up_weight: bfloat16 [32, 64, 4096], P('adapter', None, 'tensor'), may hold values from -0.75 to 0.75
- adapter_choice_index: int32 [512, 3], P(('adapter', 'dp')), may hold values from 0 to 31, as said below
Outputs:
- adapted: bfloat16 [16384, 4096], P(('adapter', 'dp'), 'tensor')
The draws below stay inside these ranges and needn't reach their ends.
Inputs may be any that keep to these rules, and one draw needn't show every extreme that they name: `adapter_choice_index`: adapter a is held by index a // 2 of the adapter axis (its owner). Among the 24 entries of the sequences of one device, at most 3 name adapters of one owner, and in every draw one owner is named exactly 3 times by the entries of every device.
All inputs are finite; a program needn't handle non-finite values.
Results may differ from the reference program's by a relative error of at most 0.02.
Values may be sent and summed in bfloat16 or wider, within the bound.
No kernel may reach another device: no remote copies, remote signals or barrier semaphores. Data moves between devices by JAX's collectives and lax.ppermute only.
A program may use at most 64 MiB of HBM per device.

```python
import jax
import jax.numpy as jnp
from jax import lax

MODEL_WIDTH = 8192
OUTPUT_FEATURES = 4096
ADAPTER_RANK = 64
ADP_DEV = 2
SEQ_LEN = 32
SEQ_DEV = 8
OWNERS = 16
BLOCKS = 64
SEQS = 512
TOKENS = 16384
ADAPTER_TOTAL = 32
CAP = 3
N_TENSOR = 8


def draw_adapter_choice_index(key, part):
    hot_key, block_key = jax.random.split(jax.random.fold_in(key, 11))
    hot_owner = jax.random.randint(hot_key, (), 0, OWNERS)
    entries = OWNERS * CAP
    pair_count = 3 * SEQ_DEV

    def one_block(block_seed):
        key_order, key_place, key_local = jax.random.split(block_seed, 3)
        owner_of = jnp.arange(entries, dtype=jnp.int32) // CAP
        shuffled = jax.random.permutation(key_order, entries).astype(jnp.int32)
        sort_score = jnp.where(owner_of == hot_owner, 0, entries).astype(jnp.int32) + shuffled
        picked = owner_of[jnp.argsort(sort_score)][:pair_count]
        picked = picked[jax.random.permutation(key_place, pair_count)]
        local_pick = jax.random.randint(key_local, (pair_count,), 0, ADP_DEV)
        return picked * ADP_DEV + local_pick
    block_keys = jax.random.split(block_key, BLOCKS)
    all_ids = jax.vmap(one_block)(block_keys)
    return all_ids.reshape(BLOCKS * SEQ_DEV, 3).astype(jnp.int32)


def level_of(own_key, shape, cuts, least, largest):
    level = 1.0
    for axis_at, blocks in cuts:
        draws = jax.random.uniform(jax.random.fold_in(jax.random.fold_in(own_key, 6), axis_at), (blocks,), jnp.float32, least / len(cuts), largest / len(cuts))
        level = level * jnp.repeat(jnp.exp(draws), shape[axis_at] // blocks).reshape((-1,) + (1,) * (len(shape) - 1 - axis_at))
    return level


def scatter_about(rng, dims, width, reach, pieces=(), kind=jnp.bfloat16):
    drawn = jax.random.normal(rng, dims, jnp.float32) * width
    if len(pieces) > 0:
        drawn = level_of(rng, dims, pieces, -0.22, 0.18) * drawn
    return jnp.clip(drawn, min=-reach, max=reach).astype(kind)


def setup_inputs(seed: int = 0) -> dict:
    seeds = jax.random.split(jax.random.key(seed), 6)
    tokens = scatter_about(seeds[0], (TOKENS, MODEL_WIDTH), 1.0, 6.0, ((0, 64), (1, 8)))
    base_projection_weight = scatter_about(seeds[1], (MODEL_WIDTH, OUTPUT_FEATURES), MODEL_WIDTH ** -0.5, 0.0625, ((0, 8), (1, 4)))
    adapter_down_weight = scatter_about(seeds[2], (ADAPTER_TOTAL, MODEL_WIDTH, ADAPTER_RANK), MODEL_WIDTH ** -0.5, 0.0625, ((0, 16), (1, 8)))
    adapter_up_weight = scatter_about(seeds[3], (ADAPTER_TOTAL, ADAPTER_RANK, OUTPUT_FEATURES), ADAPTER_RANK ** -0.5, 0.75, ((0, 16), (2, 8)))
    adapter_choice_index = draw_adapter_choice_index(jax.random.fold_in(seeds[5], 71), 0)
    return {"tokens": tokens, "base_projection_weight": base_projection_weight, "adapter_down_weight": adapter_down_weight, "adapter_up_weight": adapter_up_weight, "adapter_choice_index": adapter_choice_index}


def reference(tokens, base_projection_weight, adapter_down_weight, adapter_up_weight, adapter_choice_index):
    group_rows = MODEL_WIDTH // N_TENSOR
    base_sum = jnp.zeros((TOKENS, OUTPUT_FEATURES), jnp.float32)
    for group in range(N_TENSOR):
        group_term = jnp.dot(tokens[:, group * group_rows:(group + 1) * group_rows],
                             base_projection_weight[group * group_rows:(group + 1) * group_rows],
                             preferred_element_type=jnp.float32)
        group_term = lax.optimization_barrier(group_term.astype(jnp.bfloat16))
        base_sum = base_sum + group_term.astype(jnp.float32)
    seq_blocks = tokens.reshape(SEQS, SEQ_LEN, MODEL_WIDTH)

    def one_sequence(inputs):
        seq_rows, chosen_adapter_index = inputs
        summed = jnp.zeros((SEQ_LEN, OUTPUT_FEATURES), jnp.float32)
        for adapter_slot in range(3):
            down_projection = lax.dynamic_index_in_dim(adapter_down_weight, chosen_adapter_index[adapter_slot], 0, keepdims=False)
            up_projection = lax.dynamic_index_in_dim(adapter_up_weight, chosen_adapter_index[adapter_slot], 0, keepdims=False)
            hidden = jnp.dot(seq_rows, down_projection, preferred_element_type=jnp.float32).astype(jnp.bfloat16)
            delta_rows = jnp.dot(hidden, up_projection, preferred_element_type=jnp.float32).astype(jnp.bfloat16)
            delta_rows = lax.optimization_barrier(delta_rows)
            summed = summed + delta_rows.astype(jnp.float32)
        return summed

    adapter_total_sum = lax.map(one_sequence, (seq_blocks, adapter_choice_index))
    return (base_sum + adapter_total_sum.reshape(TOKENS, OUTPUT_FEATURES) / 3.0).astype(jnp.bfloat16)
```

```python
import jax
import jax.numpy as jnp
from jax import lax
from jax.sharding import PartitionSpec as P


def rotate(value, axis, count, step):
    return lax.ppermute(value, axis, [(i, (i - step) % count) for i in range(count)])


def swap_cores(value, count):
    return lax.ppermute(value, "tensor", [(i, i ^ 1) for i in range(count)])


def transposing_pairs(sides, step):
    pairs = []
    for x in range(sides):
        for y in range(sides):
            for core in range(2):
                target = (y + step) % sides
                pairs.append(((2 * y + core) * sides + x, (2 * x + core) * sides + target))
    return pairs


def base_output(tokens, weight):
    tensor_count = lax.axis_size("tensor")
    sides = lax.axis_size("dp")
    tensor_at = lax.axis_index("tensor")
    x = lax.axis_index("dp")
    core, y = tensor_at % 2, tensor_at // 2
    rows = tokens.shape[0]
    half = weight.shape[1] // 2
    others = [rotate(tokens, "dp", sides, step) for step in range(1, sides)]
    gathered = jnp.concatenate([tokens] + others, axis=0)
    weight_kept = lax.dynamic_slice_in_dim(weight, core * half, half, axis=1)
    weight_given = lax.dynamic_slice_in_dim(weight, (1 - core) * half, half, axis=1)
    given = jnp.dot(gathered, weight_given, preferred_element_type=jnp.float32).astype(jnp.bfloat16)
    taken = swap_cores(given, tensor_count)
    kept = jnp.dot(gathered, weight_kept, preferred_element_type=jnp.float32).astype(jnp.bfloat16)
    pair_sum = (kept.astype(jnp.float32) + taken.astype(jnp.float32)).astype(jnp.bfloat16)
    total = None
    for step in range(sides):
        block = (y + step - x + sides) % sides
        piece = lax.dynamic_slice_in_dim(pair_sum, block * rows, rows, axis=0)
        arrived = lax.ppermute(piece, ("tensor", "dp"), transposing_pairs(sides, step))
        arrived = arrived.astype(jnp.float32)
        total = arrived if total is None else total + arrived
    return total


def adapter_output(tokens, down, up, choice):
    tensor_count = lax.axis_size("tensor")
    rows = tokens.shape[0]
    per_sequence = rows // choice.shape[0]
    rank = down.shape[2]
    down_all = lax.all_gather(jnp.transpose(down, (0, 2, 1)), "adapter", axis=0, tiled=True)
    up_all = lax.all_gather(up, "adapter", axis=0, tiled=True)
    adapters = down_all.shape[0]
    down_all = down_all.reshape(adapters * rank, -1)
    up_all = up_all.reshape(adapters * rank, -1)
    choice_of_row = jnp.repeat(choice.T, per_sequence, axis=1)
    mask = choice_of_row[:, None, :] == jnp.arange(adapters, dtype=jnp.int32)[None, :, None]
    every_hidden = lax.dot_general(
        down_all, tokens, (((1,), (1,)), ((), ())), preferred_element_type=jnp.float32
    ).reshape(adapters, rank, rows)
    chosen = [
        jnp.sum(jnp.where(mask[k][:, None, :], every_hidden, 0.0), axis=0) for k in range(3)
    ]
    chosen = jnp.concatenate(chosen, axis=0).astype(jnp.bfloat16)
    pair = chosen.astype(jnp.float32) + swap_cores(chosen, tensor_count).astype(jnp.float32)
    pair = pair.astype(jnp.bfloat16)
    hidden = pair.astype(jnp.float32)
    for step in range(2, tensor_count, 2):
        hidden = hidden + rotate(pair, "tensor", tensor_count, step).astype(jnp.float32)
    hidden = hidden.astype(jnp.bfloat16).reshape(3, 1, rank, rows)
    spread = jnp.sum(
        jnp.where(mask[:, :, None, :], hidden.astype(jnp.float32), 0.0), axis=0
    ).astype(jnp.bfloat16)
    return lax.dot_general(
        spread.reshape(adapters * rank, rows),
        up_all,
        (((0,), (0,)), ((), ())),
        preferred_element_type=jnp.float32,
    )


def local(tokens, base_projection_weight, adapter_down_weight, adapter_up_weight, adapter_choice_index):
    base_sum = base_output(tokens, base_projection_weight)
    delta = adapter_output(tokens, adapter_down_weight, adapter_up_weight, adapter_choice_index)
    return (base_sum + delta / 3.0).astype(jnp.bfloat16)


def solution(mesh):
    in_specs = (
        P(("adapter", "dp"), "tensor"),
        P("tensor", "dp"),
        P("adapter", "tensor", None),
        P("adapter", None, "tensor"),
        P(("adapter", "dp"), None),
    )
    out_specs = P(("adapter", "dp"), "tensor")
    return jax.shard_map(local, mesh=mesh, in_specs=in_specs, out_specs=out_specs, check_vma=False)
```

```python
import jax
import jax.numpy as jnp
from jax import lax
from jax.sharding import PartitionSpec as P


def rotate(value, axis, count, step):
    return lax.ppermute(value, axis, [(i, (i - step) % count) for i in range(count)])


def swap_cores(value, count):
    return lax.ppermute(value, "tensor", [(i, i ^ 1) for i in range(count)])


def transposing_pairs(sides, step):
    pairs = []
    for x in range(sides):
        for y in range(sides):
            for core in range(2):
                target = (y + step) % sides
                pairs.append(((2 * y + core) * sides + x, (2 * x + core) * sides + target))
    return pairs


def base_output(gathered, weight):
    tensor_count = lax.axis_size("tensor")
    sides = lax.axis_size("dp")
    tensor_at = lax.axis_index("tensor")
    core, y = tensor_at % 2, tensor_at // 2
    rows = gathered.shape[0] // sides
    half = weight.shape[1] // 2
    weight_kept = lax.dynamic_slice_in_dim(weight, core * half, half, axis=1)
    weight_given = lax.dynamic_slice_in_dim(weight, (1 - core) * half, half, axis=1)
    given = jnp.dot(gathered, weight_given, preferred_element_type=jnp.float32).astype(jnp.bfloat16)
    taken = swap_cores(given, tensor_count)
    kept = jnp.dot(gathered, weight_kept, preferred_element_type=jnp.float32).astype(jnp.bfloat16)
    pair_sum = (kept.astype(jnp.float32) + taken.astype(jnp.float32)).astype(jnp.bfloat16)
    total = None
    for step in range(sides):
        block = (y + step) % sides
        piece = lax.dynamic_slice_in_dim(pair_sum, block * rows, rows, axis=0)
        arrived = lax.ppermute(piece, ("tensor", "dp"), transposing_pairs(sides, step))
        arrived = arrived.astype(jnp.float32)
        total = arrived if total is None else total + arrived
    return total


def choice_mask(choice, per_sequence, adapters):
    of_row = jnp.repeat(choice.T, per_sequence, axis=1)
    return of_row[:, None, None, :] == jnp.arange(adapters, dtype=jnp.int32)[None, :, None, None]


def adapter_output(gathered, down_part, up_parts, choice, choice_all):
    sides = lax.axis_size("dp")
    tensor_count = lax.axis_size("tensor")
    adapters, part, width = down_part.shape
    rows = gathered.shape[0] // sides
    per_sequence = rows // choice.shape[0]
    mask_all = choice_mask(choice_all, per_sequence, adapters)
    every_hidden = lax.dot_general(
        down_part.reshape(adapters * part, width),
        gathered,
        (((1,), (1,)), ((), ())),
        preferred_element_type=jnp.float32,
    ).reshape(adapters, part, sides * rows)
    chosen = [jnp.sum(jnp.where(mask_all[k], every_hidden, 0.0), axis=0) for k in range(3)]
    chosen = jnp.concatenate(chosen, axis=0).astype(jnp.bfloat16)
    pieces = jnp.stack([chosen[:, r * rows : (r + 1) * rows] for r in range(sides)])
    copies = jnp.broadcast_to(pieces[None], (tensor_count,) + pieces.shape)
    copies = copies.reshape((tensor_count * sides,) + pieces.shape[1:])
    arrived = lax.all_to_all(copies, ("tensor", "dp"), 0, 0, tiled=True)
    arrived = arrived.reshape(tensor_count, sides, 3, part, rows)
    hidden = sum(arrived[t].astype(jnp.float32) for t in range(tensor_count)).astype(jnp.bfloat16)
    mask = choice_mask(choice, per_sequence, adapters)
    delta = None
    for q in range(sides):
        spread = sum(
            jnp.where(mask[k], hidden[q, k][None].astype(jnp.float32), 0.0) for k in range(3)
        )
        term = lax.dot_general(
            spread.astype(jnp.bfloat16).reshape(adapters * part, rows),
            up_parts[q],
            (((0,), (0,)), ((), ())),
            preferred_element_type=jnp.float32,
        )
        delta = term if delta is None else delta + term
    return delta


def local(tokens, base_projection_weight, adapter_down_weight, adapter_up_weight, adapter_choice_index):
    sides = lax.axis_size("dp")
    owners = lax.axis_size("adapter")
    x = lax.axis_index("dp")
    held, width, rank = adapter_down_weight.shape
    rows = tokens.shape[0]
    sequences, entries = adapter_choice_index.shape
    part = rank // sides
    own_part = lax.dynamic_slice_in_dim(
        jnp.transpose(adapter_down_weight, (0, 2, 1)), x * part, part, axis=1
    ).reshape(held * part, width)
    up_parts = [
        adapter_up_weight[:, q * part : (q + 1) * part].reshape(held * part, -1)
        for q in range(sides)
    ]
    adapters = lax.all_gather(
        jnp.concatenate([own_part] + up_parts, axis=1), "adapter", axis=0, tiled=True
    )
    note = jnp.pad(
        adapter_choice_index.astype(tokens.dtype), ((0, 16 - sequences), (0, width - entries))
    )
    noted = jnp.concatenate([tokens, note], axis=0)
    gathered = jnp.zeros((sides * rows, width), tokens.dtype)
    choices = jnp.zeros((sides * sequences, entries), jnp.int32)
    for step in range(sides):
        block = noted if step == 0 else rotate(noted, "dp", sides, step)
        place = (x + step) % sides
        gathered = lax.dynamic_update_slice_in_dim(gathered, block[:rows], place * rows, axis=0)
        choice = block[rows : rows + sequences, :entries].astype(jnp.int32)
        choices = lax.dynamic_update_slice_in_dim(choices, choice, place * sequences, axis=0)
    base_sum = base_output(gathered, base_projection_weight)
    adapters, base_sum = lax.optimization_barrier((adapters, base_sum))
    down_part = adapters[:, :width].reshape(owners * held, part, width)
    up_parts = jnp.split(adapters[:, width:], sides, axis=1)
    delta = adapter_output(gathered, down_part, up_parts, adapter_choice_index, choices)
    return (base_sum + delta / 3.0).astype(jnp.bfloat16)


def solution(mesh):
    in_specs = (
        P(("adapter", "dp"), "tensor"),
        P("tensor", "dp"),
        P("adapter", "tensor", None),
        P("adapter", None, "tensor"),
        P(("adapter", "dp"), None),
    )
    out_specs = P(("adapter", "dp"), "tensor")
    return jax.shard_map(local, mesh=mesh, in_specs=in_specs, out_specs=out_specs, check_vma=False)
```

```python
import jax
import jax.numpy as jnp
from jax import lax
from jax.sharding import PartitionSpec as P


def rotate(value, axis, count, step):
    return lax.ppermute(value, axis, [(i, (i - step) % count) for i in range(count)])


def swap_cores(value, count):
    return lax.ppermute(value, "tensor", [(i, i ^ 1) for i in range(count)])


def transposing_pairs(sides, step):
    pairs = []
    for x in range(sides):
        for y in range(sides):
            for core in range(2):
                target = (y + step) % sides
                pairs.append(((2 * y + core) * sides + x, (2 * x + core) * sides + target))
    return pairs


def base_output(gathered, weight):
    tensor_count = lax.axis_size("tensor")
    sides = lax.axis_size("dp")
    tensor_at = lax.axis_index("tensor")
    core, y = tensor_at % 2, tensor_at // 2
    rows = gathered.shape[0] // sides
    half = weight.shape[1] // 2
    weight_kept = lax.dynamic_slice_in_dim(weight, core * half, half, axis=1)
    weight_given = lax.dynamic_slice_in_dim(weight, (1 - core) * half, half, axis=1)
    given = jnp.dot(gathered, weight_given, preferred_element_type=jnp.float32).astype(jnp.bfloat16)
    taken = swap_cores(given, tensor_count)
    kept = jnp.dot(gathered, weight_kept, preferred_element_type=jnp.float32).astype(jnp.bfloat16)
    pair_sum = (kept.astype(jnp.float32) + taken.astype(jnp.float32)).astype(jnp.bfloat16)
    total = None
    for step in range(sides):
        block = (y + step) % sides
        piece = lax.dynamic_slice_in_dim(pair_sum, block * rows, rows, axis=0)
        arrived = lax.ppermute(piece, ("tensor", "dp"), transposing_pairs(sides, step))
        arrived = arrived.astype(jnp.float32)
        total = arrived if total is None else total + arrived
    return total


def choice_mask(choice, per_sequence, adapters):
    of_row = jnp.repeat(choice.T, per_sequence, axis=1)
    return of_row[:, None, None, :] == jnp.arange(adapters, dtype=jnp.int32)[None, :, None, None]


def adapter_output(gathered, down_part, up_parts, choice, choice_all):
    sides = lax.axis_size("dp")
    tensor_count = lax.axis_size("tensor")
    adapters, part, width = down_part.shape
    rows = gathered.shape[0] // sides
    per_sequence = rows // choice.shape[0]
    mask_all = choice_mask(choice_all, per_sequence, adapters)
    every_hidden = lax.dot_general(
        down_part.reshape(adapters * part, width),
        gathered,
        (((1,), (1,)), ((), ())),
        preferred_element_type=jnp.float32,
    ).reshape(adapters, part, sides * rows)
    chosen = [jnp.sum(jnp.where(mask_all[k], every_hidden, 0.0), axis=0) for k in range(3)]
    chosen = jnp.concatenate(chosen, axis=0).astype(jnp.bfloat16)
    pair = chosen.astype(jnp.float32) + swap_cores(chosen, tensor_count).astype(jnp.float32)
    pair = pair.astype(jnp.bfloat16)
    pieces = jnp.stack([pair[:, r * rows : (r + 1) * rows] for r in range(sides)])
    chips = tensor_count // 2
    copies = jnp.broadcast_to(pieces[None], (chips,) + pieces.shape)
    copies = copies.reshape((chips * sides,) + pieces.shape[1:])
    groups = [
        [(2 * y + core) * sides + x for y in range(chips) for x in range(sides)]
        for core in range(2)
    ]
    arrived = lax.all_to_all(
        copies, ("tensor", "dp"), 0, 0, axis_index_groups=groups, tiled=True
    )
    arrived = arrived.reshape(chips, sides, 3, part, rows)
    hidden = sum(arrived[t].astype(jnp.float32) for t in range(chips)).astype(jnp.bfloat16)
    mask = choice_mask(choice, per_sequence, adapters)
    delta = None
    for q in range(sides):
        spread = sum(
            jnp.where(mask[k], hidden[q, k][None].astype(jnp.float32), 0.0) for k in range(3)
        )
        term = lax.dot_general(
            spread.astype(jnp.bfloat16).reshape(adapters * part, rows),
            up_parts[q],
            (((0,), (0,)), ((), ())),
            preferred_element_type=jnp.float32,
        )
        delta = term if delta is None else delta + term
    return delta


def local(tokens, base_projection_weight, adapter_down_weight, adapter_up_weight, adapter_choice_index):
    sides = lax.axis_size("dp")
    owners = lax.axis_size("adapter")
    x = lax.axis_index("dp")
    held, width, rank = adapter_down_weight.shape
    rows = tokens.shape[0]
    sequences, entries = adapter_choice_index.shape
    part = rank // sides
    own_part = lax.dynamic_slice_in_dim(
        jnp.transpose(adapter_down_weight, (0, 2, 1)), x * part, part, axis=1
    ).reshape(held * part, width)
    up_parts = [
        adapter_up_weight[:, q * part : (q + 1) * part].reshape(held * part, -1)
        for q in range(sides)
    ]
    adapters = lax.all_gather(
        jnp.concatenate([own_part] + up_parts, axis=1), "adapter", axis=0, tiled=True
    )
    note = jnp.pad(
        adapter_choice_index.astype(tokens.dtype), ((0, 16 - sequences), (0, width - entries))
    )
    noted = jnp.concatenate([tokens, note], axis=0)
    gathered = jnp.zeros((sides * rows, width), tokens.dtype)
    choices = jnp.zeros((sides * sequences, entries), jnp.int32)
    for step in range(sides):
        block = noted if step == 0 else rotate(noted, "dp", sides, step)
        place = (x + step) % sides
        gathered = lax.dynamic_update_slice_in_dim(gathered, block[:rows], place * rows, axis=0)
        choice = block[rows : rows + sequences, :entries].astype(jnp.int32)
        choices = lax.dynamic_update_slice_in_dim(choices, choice, place * sequences, axis=0)
    base_sum = base_output(gathered, base_projection_weight)
    adapters, base_sum = lax.optimization_barrier((adapters, base_sum))
    down_part = adapters[:, :width].reshape(owners * held, part, width)
    up_parts = jnp.split(adapters[:, width:], sides, axis=1)
    delta = adapter_output(gathered, down_part, up_parts, adapter_choice_index, choices)
    return (base_sum + delta / 3.0).astype(jnp.bfloat16)


def solution(mesh):
    in_specs = (
        P(("adapter", "dp"), "tensor"),
        P("tensor", "dp"),
        P("adapter", "tensor", None),
        P("adapter", None, "tensor"),
        P(("adapter", "dp"), None),
    )
    out_specs = P(("adapter", "dp"), "tensor")
    return jax.shard_map(local, mesh=mesh, in_specs=in_specs, out_specs=out_specs, check_vma=False)
```

```python
import jax
import jax.numpy as jnp
from jax import lax
from jax.sharding import PartitionSpec as P


def rotate(value, axis, count, step):
    return lax.ppermute(value, axis, [(i, (i - step) % count) for i in range(count)])


def swap_cores(value, count):
    return lax.ppermute(value, "tensor", [(i, i ^ 1) for i in range(count)])


def transposing_pairs(sides, step):
    pairs = []
    for x in range(sides):
        for y in range(sides):
            for core in range(2):
                target = (y + step) % sides
                pairs.append(((2 * y + core) * sides + x, (2 * x + core) * sides + target))
    return pairs


def base_output(gathered, weight):
    tensor_count = lax.axis_size("tensor")
    sides = lax.axis_size("dp")
    tensor_at = lax.axis_index("tensor")
    x = lax.axis_index("dp")
    core, y = tensor_at % 2, tensor_at // 2
    rows = gathered.shape[0] // sides
    half = weight.shape[1] // 2
    weight_kept = lax.dynamic_slice_in_dim(weight, core * half, half, axis=1)
    weight_given = lax.dynamic_slice_in_dim(weight, (1 - core) * half, half, axis=1)
    given = jnp.dot(gathered, weight_given, preferred_element_type=jnp.float32).astype(jnp.bfloat16)
    taken = swap_cores(given, tensor_count)
    kept = jnp.dot(gathered, weight_kept, preferred_element_type=jnp.float32).astype(jnp.bfloat16)
    pair_sum = (kept.astype(jnp.float32) + taken.astype(jnp.float32)).astype(jnp.bfloat16)
    total = None
    for step in range(sides):
        block = (y + step - x + sides) % sides
        piece = lax.dynamic_slice_in_dim(pair_sum, block * rows, rows, axis=0)
        arrived = lax.ppermute(piece, ("tensor", "dp"), transposing_pairs(sides, step))
        arrived = arrived.astype(jnp.float32)
        total = arrived if total is None else total + arrived
    return total


def choice_mask(choice, per_sequence, adapters):
    of_row = jnp.repeat(choice.T, per_sequence, axis=1)
    return of_row[:, None, None, :] == jnp.arange(adapters, dtype=jnp.int32)[None, :, None, None]


def adapter_output(gathered, down_part, up_parts, choice, choice_all):
    sides = lax.axis_size("dp")
    tensor_count = lax.axis_size("tensor")
    adapters, part, width = down_part.shape
    rows = gathered.shape[0] // sides
    per_sequence = rows // choice.shape[0]
    mask_all = choice_mask(choice_all, per_sequence, adapters)
    every_hidden = lax.dot_general(
        down_part.reshape(adapters * part, width),
        gathered,
        (((1,), (1,)), ((), ())),
        preferred_element_type=jnp.float32,
    ).reshape(adapters, part, sides * rows)
    chosen = [jnp.sum(jnp.where(mask_all[k], every_hidden, 0.0), axis=0) for k in range(3)]
    chosen = jnp.concatenate(chosen, axis=0).astype(jnp.bfloat16)
    pair = chosen.astype(jnp.float32) + swap_cores(chosen, tensor_count).astype(jnp.float32)
    pair = pair.astype(jnp.bfloat16)
    x = lax.axis_index("dp")
    pieces = jnp.stack(
        [
            lax.dynamic_slice_in_dim(pair, (r - x + sides) % sides * rows, rows, axis=1)
            for r in range(sides)
        ]
    )
    chips = tensor_count // 2
    copies = jnp.broadcast_to(pieces[None], (chips,) + pieces.shape)
    copies = copies.reshape((chips * sides,) + pieces.shape[1:])
    groups = [
        [(2 * y + core) * sides + x for y in range(chips) for x in range(sides)]
        for core in range(2)
    ]
    arrived = lax.all_to_all(
        copies, ("tensor", "dp"), 0, 0, axis_index_groups=groups, tiled=True
    )
    arrived = arrived.reshape(chips, sides, 3, part, rows)
    hidden = sum(arrived[t].astype(jnp.float32) for t in range(chips)).astype(jnp.bfloat16)
    mask = choice_mask(choice, per_sequence, adapters)
    delta = None
    for q in range(sides):
        spread = sum(
            jnp.where(mask[k], hidden[q, k][None].astype(jnp.float32), 0.0) for k in range(3)
        )
        term = lax.dot_general(
            spread.astype(jnp.bfloat16).reshape(adapters * part, rows),
            up_parts[q],
            (((0,), (0,)), ((), ())),
            preferred_element_type=jnp.float32,
        )
        delta = term if delta is None else delta + term
    return delta


def local(tokens, base_projection_weight, adapter_down_weight, adapter_up_weight, adapter_choice_index):
    sides = lax.axis_size("dp")
    owners = lax.axis_size("adapter")
    x = lax.axis_index("dp")
    held, width, rank = adapter_down_weight.shape
    rows = tokens.shape[0]
    sequences, entries = adapter_choice_index.shape
    part = rank // sides
    own_part = lax.dynamic_slice_in_dim(
        jnp.transpose(adapter_down_weight, (0, 2, 1)), x * part, part, axis=1
    ).reshape(held * part, width)
    up_parts = [
        adapter_up_weight[:, q * part : (q + 1) * part].reshape(held * part, -1)
        for q in range(sides)
    ]
    adapters = lax.all_gather(
        jnp.concatenate([own_part] + up_parts, axis=1), "adapter", axis=0, tiled=True
    )
    note = jnp.pad(
        adapter_choice_index.astype(tokens.dtype), ((0, 16 - sequences), (0, width - entries))
    )
    noted = jnp.concatenate([tokens, note], axis=0)
    blocks = [noted] + [rotate(noted, "dp", sides, step) for step in range(1, sides)]
    gathered = jnp.concatenate([tokens] + [block[:rows] for block in blocks[1:]], axis=0)
    choices = jnp.concatenate(
        [adapter_choice_index]
        + [block[rows : rows + sequences, :entries].astype(jnp.int32) for block in blocks[1:]],
        axis=0,
    )
    base_sum = base_output(gathered, base_projection_weight)
    adapters, base_sum = lax.optimization_barrier((adapters, base_sum))
    down_part = adapters[:, :width].reshape(owners * held, part, width)
    up_parts = jnp.split(adapters[:, width:], sides, axis=1)
    delta = adapter_output(gathered, down_part, up_parts, adapter_choice_index, choices)
    return (base_sum + delta / 3.0).astype(jnp.bfloat16)


def solution(mesh):
    in_specs = (
        P(("adapter", "dp"), "tensor"),
        P("tensor", "dp"),
        P("adapter", "tensor", None),
        P("adapter", None, "tensor"),
        P(("adapter", "dp"), None),
    )
    out_specs = P(("adapter", "dp"), "tensor")
    return jax.shard_map(local, mesh=mesh, in_specs=in_specs, out_specs=out_specs, check_vma=False)
```
